256 devices in a mesh: ctx: 64 (over x_lo, y, z), kvh: 4 (over x_hi, core).
Axes of the slice: x: 4 (x_hi: 2, x_lo: 2; x = x_hi * 2 + x_lo), y: 4, z: 8, core: 2. Of those that a mesh axis runs over, the one named last changes fastest.
Arguments:
- queries: bfloat16 [16384, 2048], P(('ctx', 'kvh')), may hold values from -42 to 42
- keys: bfloat16 [16384, 512], P(('ctx', 'kvh')), may hold values from -6 to 6
- values: bfloat16 [16384, 512], P(('ctx', 'kvh')), may hold values from -6 to 6
- doc_lengths: int32 [16], replicated, may hold values from 1 to 8192, 16384 in all
Outputs:
- attended: bfloat16 [16384, 2048], P(('ctx', 'kvh'))
The draws below stay inside these ranges and needn't reach their ends.
Inputs may be any that keep to these rules, and one draw needn't show every extreme that they name: `doc_lengths`: positive lengths that sum to 16384.
All inputs are finite; a program needn't handle non-finite values.
Results may differ from the reference program's by a relative error of at most 0.005.
Values may be sent and summed in bfloat16 or wider, within the bound.
No kernel may reach another device: no remote copies, remote signals or barrier semaphores. Data moves between devices by JAX's collectives and lax.ppermute only.
A program may use at most 64 MiB of HBM per device.

```python
import math
import jax
import jax.numpy as jnp
import numpy as np
from jax import lax

QUERY_HEADS = 16
KEY_VALUE_HEADS = 4
HEAD_SIZE = 128
SINK = 128
DOCS = 16
PACKED_LENGTH = 16384


def shared_sink_keys(key):
    base_offset = jnp.clip(jax.random.normal(jax.random.fold_in(key, 11), (PACKED_LENGTH, KEY_VALUE_HEADS * HEAD_SIZE), jnp.float32), -6.0, 6.0)
    return base_offset


def draw_keys(key, part):
    return shared_sink_keys(key).astype(jnp.bfloat16)


def draw_queries(key, part):
    base_offset = jnp.clip(jax.random.normal(jax.random.fold_in(key, 23), (PACKED_LENGTH, QUERY_HEADS * HEAD_SIZE), jnp.float32), -6.0, 6.0)
    return base_offset.astype(jnp.bfloat16)


def steps_of(rng, extent, cuts, smallest, largest):
    factor_of = 1.0
    for dim, shards_of in cuts:
        heights = jax.random.uniform(jax.random.fold_in(jax.random.fold_in(rng, 6), dim), (shards_of,), jnp.float32, smallest / len(cuts), largest / len(cuts))
        factor_of = factor_of * jnp.repeat(jnp.exp(heights), extent[dim] // shards_of).reshape((-1,) + (1,) * (len(extent) - 1 - dim))
    return factor_of


def profile(count, total, most, skew):
    portions = [(1 << 20) // math.isqrt(grade ** skew) + 1 for grade in range(2, count + 1)]
    spare, counts = total - most - (count - 1), [1] * (count - 1)
    while spare > 0:
        candidates = [i for i in range(count - 1) if counts[i] < most]
        whole, left = sum([portions[i] for i in candidates]), spare
        for i in candidates:
            more = min(most - counts[i], max(1, left * portions[i] // whole), spare)
            counts[i] = counts[i] + more
            spare = spare - more
    return np.array([most] + counts)


def uneven_parts(stream_key, number_of, total, reach, lean):
    if number_of == 2:
        one = jax.random.randint(stream_key, (), max(1, total - reach), min(reach, total - 1) + 1)
        return jnp.stack([one, total - one])
    sizes = jnp.asarray(profile(number_of, total, reach, lean), jnp.int32)
    pairs = (number_of - 1) // 2
    donor, receiver = sizes[1:1 + 2 * pairs:2], sizes[2:2 + 2 * pairs:2]
    room = jnp.minimum(donor - 1, reach - receiver)
    shifted = jax.random.randint(jax.random.fold_in(stream_key, 1), (pairs,), 0, 1 << 20) % (room + 1)
    sizes = sizes.at[1:1 + 2 * pairs:2].set(donor - shifted).at[2:2 + 2 * pairs:2].set(receiver + shifted)
    return sizes[jax.random.permutation(jax.random.fold_in(stream_key, 2), number_of)]


def scatter_about(own_key, extent, width, reach, cuts=(), kind=jnp.bfloat16):
    loudness = steps_of(own_key, extent, cuts, -0.22, 0.18) if cuts else 1.0
    drawn = jax.random.normal(own_key, extent, jnp.float32) * width * loudness
    return jnp.minimum(jnp.maximum(drawn, -reach), reach).astype(kind)


def setup_inputs(seed: int = 0) -> dict:
    arg_keys = jax.random.split(jax.random.key(seed), 5)
    queries = draw_queries(jax.random.fold_in(arg_keys[4], 71), 0)
    keys = draw_keys(jax.random.fold_in(arg_keys[4], 71), 0)
    values = scatter_about(arg_keys[2], (PACKED_LENGTH, KEY_VALUE_HEADS * HEAD_SIZE), 1.0, 6.0, ((0, 256),))
    doc_lengths = uneven_parts(arg_keys[3], DOCS, PACKED_LENGTH, PACKED_LENGTH // 2, 2).astype(jnp.int32)
    return {"queries": queries, "keys": keys, "values": values, "doc_lengths": doc_lengths}


def reference(queries, keys, values, doc_lengths):
    packed_sequence = queries.shape[0]
    pos = jnp.arange(packed_sequence, dtype=jnp.int32)
    starts = jnp.cumsum(doc_lengths) - doc_lengths
    doc = jnp.sum((pos[:, None] >= starts[None, :]).astype(jnp.int32), axis=1)
    allowed = (pos[None, :] <= pos[:, None]) & ((doc[:, None] == doc[None, :]) | (pos[None, :] < SINK))
    query_heads = queries.reshape(packed_sequence, QUERY_HEADS, HEAD_SIZE)
    key_head_rows = keys.reshape(packed_sequence, KEY_VALUE_HEADS, HEAD_SIZE)
    value_head_rows = values.reshape(packed_sequence, KEY_VALUE_HEADS, HEAD_SIZE)
    query_group = QUERY_HEADS // KEY_VALUE_HEADS
    scale = HEAD_SIZE ** -0.5

    def one_head(head):
        q_head = query_heads[:, head]
        k_head = key_head_rows[:, head // query_group]
        v_head = value_head_rows[:, head // query_group]
        scores = jnp.dot(q_head, k_head.T, preferred_element_type=jnp.float32) * scale
        scores = jnp.where(allowed, scores, jnp.float32(-1e30))
        rowmax = jnp.max(scores, axis=1, keepdims=True)
        expo = jnp.where(allowed, jnp.exp(scores - rowmax), jnp.float32(0.0))
        total = jnp.sum(expo, axis=1, keepdims=True)
        weights = expo.astype(jnp.bfloat16)
        return jnp.dot(weights, v_head, preferred_element_type=jnp.float32) / total

    result = lax.map(one_head, jnp.arange(QUERY_HEADS, dtype=jnp.int32))
    return jnp.transpose(result, (1, 0, 2)).reshape(packed_sequence, QUERY_HEADS * HEAD_SIZE).astype(jnp.bfloat16)
```

```python
import functools

import jax
import jax.numpy as jnp
from jax import lax
from jax.experimental import pallas as pl
from jax.experimental.pallas import tpu as pltpu
from jax.sharding import Mesh
from jax.sharding import PartitionSpec as P

HEAD = 128
SINK = 128
GROUP = ("ctx_0", "ctx_1")
RING = "ctx_2"
CTX_KVH = ("ctx_0", "ctx_1", "ctx_2", "kvh")
N_GROUPS, N_RING = 8, 8
REACH = 4
BLOCK = 256
GROUP_KEYS = N_RING * BLOCK
NEG = -1e30
LOG2E = 1.4426950408889634
SCALE = HEAD**-0.5 * LOG2E


def fill_start_of(meta_ref, q_pos):
    start = jnp.zeros(q_pos.shape, jnp.int32)
    at = jnp.int32(0)
    for i in range(15):
        at = at + meta_ref[2 + i]
        start = jnp.where(q_pos >= at, at, start)
    return start


def first_start(meta_ref, pos):
    start, at = jnp.int32(0), jnp.int32(0)
    for i in range(15):
        at = at + meta_ref[2 + i]
        start = jnp.where(pos >= at, at, start)
    return start


def attend(d, meta_ref, q_ref, *refs):
    own = d == 0
    n_in = 9 + own
    blocks, (out_ref, k_ref, v_ref, s_ref) = refs[:n_in], refs[n_in:]
    heads = q_ref.shape[1] // HEAD
    n_keys = k_ref.shape[0]
    g, z = meta_ref[0], meta_ref[1]
    q_first = (g + d) * GROUP_KEYS + z * BLOCK
    key_first = g * GROUP_KEYS
    reach = first_start(meta_ref, q_first)
    active = (g + d < N_GROUPS) & ((g == 0) | (reach < key_first + GROUP_KEYS)) if d else True

    def run():
        places = (0, 1, 7, 2, 6, 3, 5)
        v_ref[:, HEAD:] = jnp.ones((n_keys, HEAD), v_ref.dtype)
        for ref, r in zip(blocks[:7], places):
            k_ref[r * BLOCK : (r + 1) * BLOCK, :] = ref[:, :HEAD]
            v_ref[r * BLOCK : (r + 1) * BLOCK, :HEAD] = ref[:, HEAD:]
        for i, ref in enumerate(blocks[7:9]):
            at = 4 * BLOCK + i * (BLOCK // 2)
            k_ref[at : at + BLOCK // 2, :] = ref[:, :HEAD]
            v_ref[at : at + BLOCK // 2, :HEAD] = ref[:, HEAD:]
        if own:
            k_ref[GROUP_KEYS:, :] = blocks[9][:, :HEAD]
            v_ref[GROUP_KEYS:, :HEAD] = blocks[9][:, HEAD:]
        q_pos = q_first + lax.broadcasted_iota(jnp.int32, (BLOCK, 1), 0)
        start = fill_start_of(meta_ref, q_pos)
        lane = lax.broadcasted_iota(jnp.int32, (1, BLOCK), 1)
        lane_out = lax.broadcasted_iota(jnp.int32, (BLOCK, HEAD), 1)
        stats = jnp.zeros((BLOCK, HEAD), jnp.float32)
        for h in range(heads):
            cols = slice(h * HEAD, (h + 1) * HEAD)
            top = jnp.full((BLOCK, HEAD), NEG, jnp.float32)
            q = q_ref[:, cols]
            for r in range(n_keys // BLOCK + (1 if n_keys % BLOCK else 0)):
                rows = slice(r * BLOCK, min((r + 1) * BLOCK, n_keys))
                width = rows.stop - rows.start
                s = lax.dot_general(
                    q, k_ref[rows, :], (((1,), (1,)), ((), ())), preferred_element_type=jnp.float32
                )
                if r < N_RING:
                    k_pos = key_first + lax.rem(z - r + N_RING, N_RING) * BLOCK + lane
                    seen = (k_pos >= start) | (k_pos < SINK)
                    if own:
                        seen = seen & (k_pos <= q_pos)
                    s = jnp.where(seen, s, NEG)
                else:
                    s = jnp.where(g > REACH, s, NEG)
                s_ref[:, rows] = s
                for c in range(0, width, HEAD):
                    top = jnp.maximum(top, s[:, c : c + HEAD])
            m = jnp.max(top, axis=1, keepdims=True) * SCALE
            p = jnp.exp2(s_ref[...] * SCALE - m).astype(jnp.bfloat16)
            o = jnp.dot(p, v_ref[...], preferred_element_type=jnp.float32)
            total = o[:, HEAD : HEAD + 1]
            out_ref[:, cols] = (o[:, :HEAD] / o[:, HEAD:]).astype(out_ref.dtype)
            lse = m + jnp.log2(total)
            for i in range(1 if own else 3):
                word = lse if own else lse.astype(jnp.bfloat16).astype(jnp.float32)
                stats = jnp.where(lane_out == 3 * h + i, word, stats)
                lse = lse - word
        out_ref[:, heads * HEAD :] = stats.astype(out_ref.dtype)

    if own:
        run()
    else:
        pl.when(active)(run)

        @pl.when(jnp.logical_not(active))
        def _():
            out_ref[:, : heads * HEAD] = jnp.zeros((BLOCK, heads * HEAD), out_ref.dtype)
            lane_out = lax.broadcasted_iota(jnp.int32, (BLOCK, HEAD), 1)
            out_ref[:, heads * HEAD :] = jnp.where(lane_out % 3 == 0, NEG, 0.0).astype(out_ref.dtype)


def merge(meta_ref, own_ref, *refs):
    parts, out_ref = refs[:REACH], refs[REACH]
    g = meta_ref[0]
    heads = out_ref.shape[1] // HEAD
    base = heads * HEAD
    for h in range(heads):
        cols = slice(h * HEAD, (h + 1) * HEAD)
        lses = [own_ref[:, base + 3 * h : base + 3 * h + 1]]
        for d, ref in enumerate(parts, 1):
            words = ref[:, base:].astype(jnp.float32)
            lse = words[:, 3 * h : 3 * h + 1] + words[:, 3 * h + 1 : 3 * h + 2] + words[:, 3 * h + 2 : 3 * h + 3]
            lses.append(jnp.where(g >= d, lse, NEG))
        top = functools.reduce(jnp.maximum, lses)
        weights = [jnp.exp2(x - top) for x in lses]
        total = functools.reduce(jnp.add, weights)
        acc = own_ref[:, cols] * (weights[0] / total)
        for w, ref in zip(weights[1:], parts):
            acc = acc + ref[:, cols].astype(jnp.float32) * (w / total)
        out_ref[:, cols] = acc.astype(out_ref.dtype)


VMEM = pl.BlockSpec(memory_space=pltpu.VMEM)
SMEM = pl.BlockSpec(memory_space=pltpu.SMEM)


def attend_call(d, meta, q, blocks):
    n_keys = GROUP_KEYS + (SINK if d == 0 else 0)
    width = q.shape[1]
    return pl.pallas_call(
        functools.partial(attend, d),
        name=f"attend_{d}",
        out_shape=jax.ShapeDtypeStruct((BLOCK, width + HEAD), jnp.float32 if d == 0 else jnp.bfloat16),
        in_specs=[SMEM] + [VMEM] * (1 + len(blocks)),
        out_specs=VMEM,
        scratch_shapes=[
            pltpu.VMEM((n_keys, HEAD), jnp.bfloat16),
            pltpu.VMEM((n_keys, 2 * HEAD), jnp.bfloat16),
            pltpu.VMEM((BLOCK, n_keys), jnp.float32),
        ],
        compiler_params=pltpu.CompilerParams(vmem_limit_bytes=24 << 20),
        cost_estimate=pl.CostEstimate(
            flops=6 * BLOCK * n_keys * width,
            transcendentals=BLOCK * n_keys * width // HEAD,
            bytes_accessed=4 << 20,
        ),
    )(meta, q, *blocks)


def merge_call(meta, own, parts):
    width = own.shape[1] - HEAD
    return pl.pallas_call(
        merge,
        name="merge",
        out_shape=jax.ShapeDtypeStruct((BLOCK, width), jnp.bfloat16),
        in_specs=[SMEM] + [VMEM] * (1 + len(parts)),
        out_specs=VMEM,
        compiler_params=pltpu.CompilerParams(vmem_limit_bytes=16 << 20),
    )(meta, own, *parts)


def along_ring(x, step):
    return lax.ppermute(x, RING, [(i, (i + step) % N_RING) for i in range(N_RING)])


def to_group(x, step):
    return lax.ppermute(x, GROUP, [(i, i + step) for i in range(N_GROUPS) if 0 <= i + step < N_GROUPS])


def shards(queries, keys, values, doc_lengths):
    rows = queries.shape[0]
    kv_heads = keys.shape[1] // HEAD
    by_head = jnp.concatenate([x.reshape(rows, kv_heads, -1) for x in (queries, keys, values)], axis=2)
    mine = lax.all_to_all(by_head.reshape(rows, -1), "kvh", split_axis=1, concat_axis=0, tiled=True)
    width = queries.shape[1] // kv_heads
    q, kv = mine[:, :width], mine[:, width:]
    g, z = lax.axis_index(GROUP), lax.axis_index(RING)
    meta = jnp.concatenate([jnp.stack([g, z]).astype(jnp.int32), doc_lengths])

    half = BLOCK // 2
    visiting = {}
    blocks, up, down = [kv], kv, kv
    for step in range(3):
        up, down = along_ring(up, 1), along_ring(down, -1)
        visiting[REACH - step] = to_group(q, step - REACH)
        blocks += [up, down]
    blocks += [along_ring(up[:half], 1), along_ring(down[half:], -1)]
    visiting[1] = to_group(q, -1)

    held = jnp.stack([b[:half] for b in blocks[:7]] + [blocks[7]])
    place = jnp.array([0, 1, 3, 5, 7, 6, 4, 2])[z]
    first = lax.dynamic_index_in_dim(held, place, 0, keepdims=False)
    sink = first * 0
    for far in range(REACH + 1, N_GROUPS):
        got = lax.ppermute(first, GROUP, [(0, far)])
        sink = jnp.where(g == far, got, sink)

    parts = []
    for d in range(REACH, 0, -1):
        parts.insert(0, to_group(attend_call(d, meta, visiting[d], blocks), d))
    own = attend_call(0, meta, q, blocks + [sink])
    out = merge_call(meta, own, parts)
    return lax.all_to_all(out, "kvh", split_axis=0, concat_axis=1, tiled=True)


def solution(mesh):
    torus = Mesh(mesh.devices.reshape(2, 4, 8, mesh.shape["kvh"]), CTX_KVH)
    in_specs = (P(CTX_KVH, None), P(CTX_KVH, None), P(CTX_KVH, None), P())
    return jax.shard_map(
        shards, mesh=torus, in_specs=in_specs, out_specs=P(CTX_KVH, None), check_vma=False
    )
```

```python
import functools

import jax
import jax.numpy as jnp
from jax import lax
from jax.experimental import pallas as pl
from jax.experimental.pallas import tpu as pltpu
from jax.sharding import Mesh
from jax.sharding import PartitionSpec as P

HEAD = 128
SINK = 128
GROUP = ("ctx_0", "ctx_1")
RING = "ctx_2"
CTX_KVH = ("ctx_0", "ctx_1", "ctx_2", "kvh")
N_GROUPS, N_RING = 8, 8
REACH = 4
BLOCK = 256
GROUP_KEYS = N_RING * BLOCK
NEG = -1e30
LOG2E = 1.4426950408889634
SCALE = HEAD**-0.5 * LOG2E


LOW, HIGH = 2.0**-96, 2.0**96
LANES = 128
GATE = 24
NT = (((1,), (1,)), ((), ()))


def document_bounds(meta_ref):
    lane = lax.broadcasted_iota(jnp.int32, (1, LANES), 1)
    first, end = jnp.zeros((1, LANES), jnp.int32), jnp.zeros((1, LANES), jnp.int32)
    at = jnp.int32(0)
    for i in range(16):
        first = jnp.where(lane == i, at, first)
        at = at + meta_ref[2 + i]
        end = jnp.where(lane == i, at, end)
    return first, end


def start_of(meta_ref, pos):
    start, at = jnp.zeros_like(pos), jnp.int32(0)
    for i in range(15):
        at = at + meta_ref[2 + i]
        start = jnp.where(pos >= at, at, start)
    return start


def assemble(meta_ref, *refs):
    blocks, (k_ref, v_ref) = refs[:9], refs[9:]
    g, z = meta_ref[0], meta_ref[1]
    first, end = document_bounds(meta_ref)
    lane = lax.broadcasted_iota(jnp.int32, (1, LANES), 1)
    half = BLOCK // 2
    pieces = [(r * BLOCK, r, 0, ref) for ref, r in zip(blocks[:7], (0, 1, 7, 2, 6, 3, 5))]
    pieces += [(4 * BLOCK, 4, 0, blocks[7]), (4 * BLOCK + half, 4, half, blocks[8])]
    for at, r, offset, ref in pieces:
        n = ref.shape[0]
        block = lax.rem(z - r + N_RING, N_RING)
        pos = g * GROUP_KEYS + block * BLOCK + offset + lax.broadcasted_iota(jnp.int32, (n, 1), 0)
        seen = ((pos >= first) & (pos < end)) | (pos < SINK)
        k_ref[at : at + n, :HEAD] = ref[:, :HEAD]
        k_ref[at : at + n, HEAD:] = jnp.where(seen, 0.0, NEG).astype(k_ref.dtype)
        v_ref[at : at + n, :HEAD] = ref[:, HEAD:]
        v_ref[at : at + n, HEAD:] = jnp.ones((n, HEAD), v_ref.dtype)


def query_columns(meta_ref, q_first):
    first, end = document_bounds(meta_ref)
    pos = q_first + lax.broadcasted_iota(jnp.int32, (BLOCK, 1), 0)
    return jnp.where((pos >= first) & (pos < end), 1.0, 0.0).astype(jnp.bfloat16)


def scores(q, k):
    return lax.dot_general(q, k, NT, preferred_element_type=jnp.float32)


def finish(out_ref, h, o, m, stats):
    total = o[:, HEAD:]
    some = total > 0.0
    cols = slice(h * HEAD, (h + 1) * HEAD)
    out_ref[:BLOCK, cols] = (o[:, :HEAD] / jnp.where(some, total, 1.0)).astype(out_ref.dtype)
    lse = m + jnp.where(some, jnp.log2(total), NEG)
    lane = lax.broadcasted_iota(jnp.int32, lse.shape, 1)
    for i in range(3):
        word = lse.astype(jnp.bfloat16).astype(jnp.float32)
        stats = jnp.where(lane == 4 * i + h, word, stats)
        lse = lse - word
    return stats


def put_stats(out_ref, stats):
    rows = stats.T[:16]
    out_ref[BLOCK:, :BLOCK] = rows.astype(out_ref.dtype)
    out_ref[BLOCK:, BLOCK:] = jnp.zeros((16, out_ref.shape[1] - BLOCK), out_ref.dtype)


def in_range(o, visible):
    total = o[:, HEAD:]
    return jnp.where(visible & jnp.logical_not((total >= LOW) & (total <= HIGH)), 1.0, 0.0)


def attend_visitor(d, meta_ref, q_ref, k_ref, v_ref, out_ref, p_ref):
    heads = q_ref.shape[1] // HEAD
    g, z = meta_ref[0], meta_ref[1]
    q_first = (g + d) * GROUP_KEYS + z * BLOCK
    key_end = (g + 1) * GROUP_KEYS
    active = (g + d < N_GROUPS) & ((g == 0) | (start_of(meta_ref, q_first) < key_end))

    @pl.when(active)
    def _():
        mask = query_columns(meta_ref, q_first)
        pos = q_first + lax.broadcasted_iota(jnp.int32, (BLOCK, 1), 0)
        visible = (start_of(meta_ref, pos) < key_end) | (g == 0)
        stats = jnp.zeros((BLOCK, LANES), jnp.float32)
        off = jnp.zeros((BLOCK, LANES), jnp.float32)
        for h in range(heads):
            q = jnp.concatenate([q_ref[:, h * HEAD : (h + 1) * HEAD], mask], axis=1)
            for r in range(0, GROUP_KEYS, BLOCK):
                s = scores(q, k_ref[r : r + BLOCK, :])
                p_ref[h % 2, :, r : r + BLOCK] = jnp.exp2(s * SCALE).astype(jnp.bfloat16)
            o = jnp.dot(p_ref[h % 2], v_ref[...], preferred_element_type=jnp.float32)
            off = jnp.maximum(off, in_range(o, visible))
            stats = finish(out_ref, h, o, 0.0, stats)
        put_stats(out_ref, stats)

        @pl.when(jnp.max(off) > 0.0)
        def _():
            stats = jnp.zeros((BLOCK, LANES), jnp.float32)
            for h in range(heads):
                q = jnp.concatenate([q_ref[:, h * HEAD : (h + 1) * HEAD], mask], axis=1)

                def highest(r, top):
                    rows = pl.ds(pl.multiple_of(r * BLOCK, BLOCK), BLOCK)
                    return jnp.maximum(top, jnp.max(scores(q, k_ref[rows, :]), axis=1, keepdims=True))

                m = lax.fori_loop(0, N_RING, highest, jnp.full((BLOCK, 1), 2 * NEG, jnp.float32))

                def weigh(r, o):
                    rows = pl.ds(pl.multiple_of(r * BLOCK, BLOCK), BLOCK)
                    p = jnp.exp2((scores(q, k_ref[rows, :]) - m) * SCALE).astype(jnp.bfloat16)
                    return o + jnp.dot(p, v_ref[rows, :], preferred_element_type=jnp.float32)

                o = lax.fori_loop(0, N_RING, weigh, jnp.zeros((BLOCK, 2 * HEAD), jnp.float32))
                stats = finish(out_ref, h, o, m * SCALE, stats)
            put_stats(out_ref, stats)

    @pl.when(jnp.logical_not(active))
    def _():
        out_ref[:BLOCK, :] = jnp.zeros((BLOCK, q_ref.shape[1]), out_ref.dtype)
        out_ref[BLOCK:, :] = jnp.full((16, q_ref.shape[1]), NEG, out_ref.dtype)


def attend_own(meta_ref, q_ref, k_ref, v_ref, sink_ref, out_ref, acc_ref):
    heads = q_ref.shape[1] // HEAD
    g, z = meta_ref[0], meta_ref[1]
    q_first = g * GROUP_KEYS + z * BLOCK
    mask = query_columns(meta_ref, q_first)
    row = lax.broadcasted_iota(jnp.int32, (BLOCK, BLOCK), 0)
    column = lax.broadcasted_iota(jnp.int32, (BLOCK, BLOCK), 1)
    far = g > REACH

    def query(h):
        return jnp.concatenate([q_ref[:, h * HEAD : (h + 1) * HEAD], mask], axis=1)

    def own_scores(h):
        return jnp.where(column <= row, scores(query(h), k_ref[:BLOCK, :]), NEG)

    def sink_scores(h):
        return scores(q_ref[:, h * HEAD : (h + 1) * HEAD], sink_ref[:, :HEAD])

    sink_v = jnp.concatenate([sink_ref[:, HEAD:], jnp.ones((SINK, HEAD), sink_ref.dtype)], axis=1)

    def weighted(s, m, v):
        p = jnp.exp2((s - m) * SCALE).astype(jnp.bfloat16)
        return jnp.dot(p, v, preferred_element_type=jnp.float32)

    def store_all(ms):
        stats = jnp.zeros((BLOCK, LANES), jnp.float32)
        for h in range(heads):
            stats = finish(out_ref, h, acc_ref[h], ms[h] * SCALE, stats)
        put_stats(out_ref, stats)

    def sweep(ms):
        for h in range(heads):
            acc_ref[h] = weighted(own_scores(h), ms[h], v_ref[:BLOCK, :])
        for r in range(1, N_RING):

            @pl.when(r <= z)
            def _():
                rows = slice(r * BLOCK, (r + 1) * BLOCK)
                for h in range(heads):
                    acc_ref[h] += weighted(scores(query(h), k_ref[rows, :]), ms[h], v_ref[rows, :])

        @pl.when(far)
        def _():
            for h in range(heads):
                acc_ref[h] += weighted(sink_scores(h), ms[h], sink_v)

    sweep([0.0] * heads)
    store_all([0.0] * heads)
    off = in_range(acc_ref[0], True)
    for h in range(1, heads):
        off = jnp.maximum(off, in_range(acc_ref[h], True))

    @pl.when(jnp.max(off) > 0.0)
    def _():
        ms = []
        for h in range(heads):
            top = jnp.max(own_scores(h), axis=1, keepdims=True)

            def highest(r, top):
                rows = pl.ds(pl.multiple_of(r * BLOCK, BLOCK), BLOCK)
                return jnp.maximum(top, jnp.max(scores(query(h), k_ref[rows, :]), axis=1, keepdims=True))

            top = lax.fori_loop(1, z + 1, highest, top)
            ms.append(jnp.where(far, jnp.maximum(top, jnp.max(sink_scores(h), axis=1, keepdims=True)), top))
        sweep(ms)
        store_all(ms)


def merge(meta_ref, own_ref, *refs):
    parts, out_ref = refs[:REACH], refs[REACH]
    g = meta_ref[0]
    heads = out_ref.shape[1] // HEAD

    def lse_of(ref):
        words = ref[BLOCK:, :BLOCK].astype(jnp.float32)
        return words[0:4] + words[4:8] + words[8:12]

    lses = [lse_of(own_ref)] + [jnp.where(g >= d, lse_of(ref), NEG) for d, ref in enumerate(parts, 1)]
    top = functools.reduce(jnp.maximum, lses)
    weights = [jnp.exp2(x - top) for x in lses]
    total = functools.reduce(jnp.add, weights)
    rows = [w / total for w in weights]
    rows.append(jnp.zeros((LANES - heads * (REACH + 1), BLOCK), jnp.float32))
    columns = jnp.concatenate(rows, axis=0).T
    for h in range(heads):
        cols = slice(h * HEAD, (h + 1) * HEAD)
        acc = own_ref[:BLOCK, cols] * columns[:, h : h + 1]
        for d, ref in enumerate(parts, 1):
            acc = acc + ref[:BLOCK, cols].astype(jnp.float32) * columns[:, heads * d + h : heads * d + h + 1]
        out_ref[:, cols] = acc.astype(out_ref.dtype)


VMEM = pl.BlockSpec(memory_space=pltpu.VMEM)
SMEM = pl.BlockSpec(memory_space=pltpu.SMEM)


def assemble_call(meta, blocks):
    return pl.pallas_call(
        assemble,
        name="assemble",
        out_shape=[jax.ShapeDtypeStruct((GROUP_KEYS, 2 * HEAD), jnp.bfloat16)] * 2,
        in_specs=[SMEM] + [VMEM] * len(blocks),
        out_specs=[VMEM, VMEM],
        compiler_params=pltpu.CompilerParams(vmem_limit_bytes=12 << 20),
        cost_estimate=pl.CostEstimate(flops=1 << 20, transcendentals=0, bytes_accessed=3 << 20),
    )(meta, *blocks)


def cost(width):
    return pl.CostEstimate(
        flops=8 * BLOCK * GROUP_KEYS * width,
        transcendentals=BLOCK * GROUP_KEYS * width // HEAD,
        bytes_accessed=3 << 20,
    )


def visitor_call(d, meta, q, k, v):
    width = q.shape[1]
    return pl.pallas_call(
        functools.partial(attend_visitor, d),
        name=f"attend_{d}",
        out_shape=jax.ShapeDtypeStruct((BLOCK + 16, width), jnp.bfloat16),
        in_specs=[SMEM] + [VMEM] * 3,
        out_specs=VMEM,
        scratch_shapes=[pltpu.VMEM((2, BLOCK, GROUP_KEYS), jnp.bfloat16)],
        compiler_params=pltpu.CompilerParams(vmem_limit_bytes=20 << 20),
        cost_estimate=cost(width),
    )(meta, q, k, v)


def own_call(meta, q, k, v, sink):
    width = q.shape[1]
    return pl.pallas_call(
        attend_own,
        name="attend_0",
        out_shape=jax.ShapeDtypeStruct((BLOCK + 16, width), jnp.float32),
        in_specs=[SMEM] + [VMEM] * 4,
        out_specs=VMEM,
        scratch_shapes=[pltpu.VMEM((width // HEAD, BLOCK, 2 * HEAD), jnp.float32)],
        compiler_params=pltpu.CompilerParams(vmem_limit_bytes=20 << 20),
        cost_estimate=cost(width),
    )(meta, q, k, v, sink)


def merge_call(meta, own, parts):
    return pl.pallas_call(
        merge,
        name="merge",
        out_shape=jax.ShapeDtypeStruct((BLOCK, own.shape[1]), jnp.bfloat16),
        in_specs=[SMEM] + [VMEM] * (1 + len(parts)),
        out_specs=VMEM,
        compiler_params=pltpu.CompilerParams(vmem_limit_bytes=16 << 20),
    )(meta, own, *parts)


def along_ring(x, step):
    return lax.ppermute(x, RING, [(i, (i + step) % N_RING) for i in range(N_RING)])


def to_group(x, step):
    return lax.ppermute(x, GROUP, [(i, i + step) for i in range(N_GROUPS) if 0 <= i + step < N_GROUPS])


def shards(queries, keys, values, doc_lengths):
    rows = queries.shape[0]
    kv_heads = keys.shape[1] // HEAD
    by_head = jnp.concatenate([x.reshape(rows, kv_heads, -1) for x in (queries, keys, values)], axis=2)
    mine = lax.all_to_all(by_head.reshape(rows, -1), "kvh", split_axis=1, concat_axis=0, tiled=True)
    width = queries.shape[1] // kv_heads
    q, kv = mine[:, :width], mine[:, width:]
    g, z = lax.axis_index(GROUP), lax.axis_index(RING)
    meta = jnp.concatenate([jnp.stack([g, z]).astype(jnp.int32), doc_lengths])

    half = BLOCK // 2
    visiting = {}
    blocks, up, down = [kv], kv, kv
    for step in range(3):
        up, down = along_ring(up, 1), along_ring(down, -1)
        visiting[REACH - step] = to_group(q, step - REACH)
        blocks += [up, down]
    blocks += [along_ring(up[:half], 1), along_ring(down[half:], -1)]
    visiting[1] = to_group(q, -1)

    first = blocks[0][:half]
    for r, i in enumerate((1, 3, 5, 7, 6, 4, 2), 1):
        first = jnp.where(z == r, blocks[i][:half], first)
    sink = jnp.zeros_like(first)
    for far in range(REACH + 1, N_GROUPS):
        got = lax.ppermute(first, GROUP, [(0, far)])
        sink = jnp.where(g == far, got, sink)

    k, v = assemble_call(meta, blocks)
    parts = []
    for d in range(REACH, 0, -1):
        parts.insert(0, to_group(visitor_call(d, meta, visiting[d], k, v), d))
    own = own_call(meta, q, k, v, sink)
    out = merge_call(meta, own, parts)
    return lax.all_to_all(out, "kvh", split_axis=0, concat_axis=1, tiled=True)


def solution(mesh):
    torus = Mesh(mesh.devices.reshape(2, 4, 8, mesh.shape["kvh"]), CTX_KVH)
    in_specs = (P(CTX_KVH, None), P(CTX_KVH, None), P(CTX_KVH, None), P())
    return jax.shard_map(
        shards, mesh=torus, in_specs=in_specs, out_specs=P(CTX_KVH, None), check_vma=False
    )
```

```python
import functools

import jax
import jax.numpy as jnp
from jax import lax
from jax.experimental import pallas as pl
from jax.experimental.pallas import tpu as pltpu
from jax.sharding import Mesh
from jax.sharding import PartitionSpec as P

HEAD = 128
SINK = 128
GROUP = ("ctx_0", "ctx_1")
RING = "ctx_2"
CTX_KVH = ("ctx_0", "ctx_1", "ctx_2", "kvh")
N_GROUPS, N_RING = 8, 8
REACH = 4
BLOCK = 256
GROUP_KEYS = N_RING * BLOCK
NEG = -1e30
LOG2E = 1.4426950408889634
SCALE = HEAD**-0.5 * LOG2E


LOW, HIGH = 2.0**-96, 2.0**96
LANES = 128
GATE = 24
NT = (((1,), (1,)), ((), ()))


def document_bounds(meta_ref):
    lane = lax.broadcasted_iota(jnp.int32, (1, LANES), 1)
    first, end = jnp.zeros((1, LANES), jnp.int32), jnp.zeros((1, LANES), jnp.int32)
    at = jnp.int32(0)
    for i in range(16):
        first = jnp.where(lane == i, at, first)
        at = at + meta_ref[2 + i]
        end = jnp.where(lane == i, at, end)
    return first, end


def start_of(meta_ref, pos):
    start, at = jnp.zeros_like(pos), jnp.int32(0)
    for i in range(15):
        at = at + meta_ref[2 + i]
        start = jnp.where(pos >= at, at, start)
    return start


def assemble(meta_ref, *refs):
    blocks, (k_ref, v_ref) = refs[:9], refs[9:]
    g, z = meta_ref[0], meta_ref[1]
    first, end = document_bounds(meta_ref)
    lane = lax.broadcasted_iota(jnp.int32, (1, LANES), 1)
    half = BLOCK // 2
    pieces = [(r * BLOCK, r, 0, ref) for ref, r in zip(blocks[:7], (0, 1, 7, 2, 6, 3, 5))]
    pieces += [(4 * BLOCK, 4, 0, blocks[7]), (4 * BLOCK + half, 4, half, blocks[8])]
    for at, r, offset, ref in pieces:
        n = ref.shape[0]
        block = lax.rem(z - r + N_RING, N_RING)
        pos = g * GROUP_KEYS + block * BLOCK + offset + lax.broadcasted_iota(jnp.int32, (n, 1), 0)
        seen = ((pos >= first) & (pos < end)) | (pos < SINK)
        k_ref[at : at + n, :HEAD] = ref[:, :HEAD]
        k_ref[at : at + n, HEAD:] = jnp.where(seen, 0.0, NEG).astype(k_ref.dtype)
        v_ref[at : at + n, :HEAD] = ref[:, HEAD:]
        v_ref[at : at + n, HEAD:] = jnp.ones((n, HEAD), v_ref.dtype)


def query_columns(meta_ref, q_first):
    first, end = document_bounds(meta_ref)
    pos = q_first + lax.broadcasted_iota(jnp.int32, (BLOCK, 1), 0)
    return jnp.where((pos >= first) & (pos < end), 1.0, 0.0).astype(jnp.bfloat16)


def scores(q, k):
    return lax.dot_general(q, k, NT, preferred_element_type=jnp.float32)


def columns_of(h):
    return pl.ds(pl.multiple_of(h * HEAD, HEAD), HEAD)


def finish(out_ref, stats_ref, h, o, m):
    total = o[:, HEAD:]
    some = total > 0.0
    out_ref[:BLOCK, columns_of(h)] = (o[:, :HEAD] / jnp.where(some, total, 1.0)).astype(out_ref.dtype)
    lse = m + jnp.where(some, jnp.log2(total), NEG)
    lane = lax.broadcasted_iota(jnp.int32, lse.shape, 1)
    stats = stats_ref[...]
    for i in range(3):
        word = lse.astype(jnp.bfloat16).astype(jnp.float32)
        stats = jnp.where(lane == 4 * i + h, word, stats)
        lse = lse - word
    stats_ref[...] = stats


def put_stats(out_ref, stats_ref):
    rows = stats_ref[...].T[:16]
    out_ref[BLOCK:, :BLOCK] = rows.astype(out_ref.dtype)
    out_ref[BLOCK:, BLOCK:] = jnp.zeros((16, out_ref.shape[1] - BLOCK), out_ref.dtype)


def note_range(off_ref, o, visible):
    total = o[:, HEAD:]
    off = jnp.where(visible & jnp.logical_not((total >= LOW) & (total <= HIGH)), 1.0, 0.0)
    off_ref[...] = jnp.maximum(off_ref[...], off)


def rows_of(r):
    return pl.ds(pl.multiple_of(r * BLOCK, BLOCK), BLOCK)


def weighted(s, m, v):
    p = jnp.exp2((s if m is None else s - m) * SCALE).astype(jnp.bfloat16)
    return jnp.dot(p, v, preferred_element_type=jnp.float32)


def each_head(heads, body):
    lax.fori_loop(0, heads, lambda h, _: (body(h), 0)[1], 0)


def attend_visitor(d, meta_ref, q_ref, k_ref, v_ref, out_ref, p_ref, stats_ref, off_ref):
    heads = q_ref.shape[1] // HEAD
    g, z = meta_ref[0], meta_ref[1]
    q_first = (g + d) * GROUP_KEYS + z * BLOCK
    key_end = (g + 1) * GROUP_KEYS
    active = (g + d < N_GROUPS) & ((g == 0) | (start_of(meta_ref, q_first) < key_end))

    @pl.when(active)
    def _():
        mask = query_columns(meta_ref, q_first)
        pos = q_first + lax.broadcasted_iota(jnp.int32, (BLOCK, 1), 0)
        visible = (start_of(meta_ref, pos) < key_end) | (g == 0)
        stats_ref[...] = jnp.zeros((BLOCK, LANES), jnp.float32)
        off_ref[...] = jnp.zeros((BLOCK, LANES), jnp.float32)

        def query(h):
            return jnp.concatenate([q_ref[:, columns_of(h)], mask], axis=1)

        def plain(h):
            q = query(h)
            for r in range(0, GROUP_KEYS, BLOCK):
                s = scores(q, k_ref[r : r + BLOCK, :])
                p_ref[:, r : r + BLOCK] = jnp.exp2(s * SCALE).astype(jnp.bfloat16)
            o = jnp.dot(p_ref[...], v_ref[...], preferred_element_type=jnp.float32)
            note_range(off_ref, o, visible)
            finish(out_ref, stats_ref, h, o, 0.0)

        each_head(heads, plain)
        put_stats(out_ref, stats_ref)

        @pl.when(jnp.max(off_ref[...]) > 0.0)
        def _():
            def careful(h):
                q = query(h)

                def highest(r, top):
                    return jnp.maximum(top, jnp.max(scores(q, k_ref[rows_of(r), :]), axis=1, keepdims=True))

                m = lax.fori_loop(0, N_RING, highest, jnp.full((BLOCK, 1), 2 * NEG, jnp.float32))
                o = lax.fori_loop(
                    0,
                    N_RING,
                    lambda r, o: o + weighted(scores(q, k_ref[rows_of(r), :]), m, v_ref[rows_of(r), :]),
                    jnp.zeros((BLOCK, 2 * HEAD), jnp.float32),
                )
                finish(out_ref, stats_ref, h, o, m * SCALE)

            each_head(heads, careful)
            put_stats(out_ref, stats_ref)

    @pl.when(jnp.logical_not(active))
    def _():
        out_ref[:BLOCK, :] = jnp.zeros((BLOCK, q_ref.shape[1]), out_ref.dtype)
        out_ref[BLOCK:, :] = jnp.full((16, q_ref.shape[1]), NEG, out_ref.dtype)


def attend_own(meta_ref, q_ref, k_ref, v_ref, sink_ref, out_ref, acc_ref, stats_ref, off_ref):
    heads = q_ref.shape[1] // HEAD
    g, z = meta_ref[0], meta_ref[1]
    q_first = g * GROUP_KEYS + z * BLOCK
    mask = query_columns(meta_ref, q_first)
    row = lax.broadcasted_iota(jnp.int32, (BLOCK, BLOCK), 0)
    column = lax.broadcasted_iota(jnp.int32, (BLOCK, BLOCK), 1)
    far = g > REACH
    stats_ref[...] = jnp.zeros((BLOCK, LANES), jnp.float32)
    off_ref[...] = jnp.zeros((BLOCK, LANES), jnp.float32)

    def own_scores(q):
        return jnp.where(column <= row, scores(q, k_ref[:BLOCK, :]), NEG)

    def sink_scores(q):
        return scores(q[:, :HEAD], sink_ref[:, :HEAD])

    def attend(h, exact):
        q = jnp.concatenate([q_ref[:, columns_of(h)], mask], axis=1)
        m = None
        if exact:
            m = jnp.max(own_scores(q), axis=1, keepdims=True)
            m = lax.fori_loop(
                1,
                z + 1,
                lambda r, m: jnp.maximum(m, jnp.max(scores(q, k_ref[rows_of(r), :]), axis=1, keepdims=True)),
                m,
            )
            m = jnp.where(far, jnp.maximum(m, jnp.max(sink_scores(q), axis=1, keepdims=True)), m)
        acc_ref[...] = weighted(own_scores(q), m, v_ref[:BLOCK, :])

        def add(r, _):
            acc_ref[...] += weighted(scores(q, k_ref[rows_of(r), :]), m, v_ref[rows_of(r), :])
            return 0

        lax.fori_loop(1, z + 1, add, 0)

        @pl.when(far)
        def _():
            sink_v = jnp.concatenate([sink_ref[:, HEAD:], jnp.ones((SINK, HEAD), sink_ref.dtype)], axis=1)
            acc_ref[...] += weighted(sink_scores(q), m, sink_v)

        o = acc_ref[...]
        if not exact:
            note_range(off_ref, o, True)
        finish(out_ref, stats_ref, h, o, m * SCALE if exact else 0.0)

    each_head(heads, lambda h: attend(h, False))
    put_stats(out_ref, stats_ref)

    @pl.when(jnp.max(off_ref[...]) > 0.0)
    def _():
        each_head(heads, lambda h: attend(h, True))
        put_stats(out_ref, stats_ref)


def merge(meta_ref, own_ref, *refs):
    parts, out_ref = refs[:REACH], refs[REACH]
    g = meta_ref[0]
    heads = out_ref.shape[1] // HEAD

    def lse_of(ref):
        words = ref[BLOCK:, :BLOCK].astype(jnp.float32)
        return words[0:4] + words[4:8] + words[8:12]

    lses = [lse_of(own_ref)] + [jnp.where(g >= d, lse_of(ref), NEG) for d, ref in enumerate(parts, 1)]
    top = functools.reduce(jnp.maximum, lses)
    weights = [jnp.exp2(x - top) for x in lses]
    total = functools.reduce(jnp.add, weights)
    rows = [w / total for w in weights]
    rows.append(jnp.zeros((LANES - heads * (REACH + 1), BLOCK), jnp.float32))
    columns = jnp.concatenate(rows, axis=0).T
    for h in range(heads):
        cols = slice(h * HEAD, (h + 1) * HEAD)
        acc = own_ref[:BLOCK, cols] * columns[:, h : h + 1]
        for d, ref in enumerate(parts, 1):
            acc = acc + ref[:BLOCK, cols].astype(jnp.float32) * columns[:, heads * d + h : heads * d + h + 1]
        out_ref[:, cols] = acc.astype(out_ref.dtype)


VMEM = pl.BlockSpec(memory_space=pltpu.VMEM)
SMEM = pl.BlockSpec(memory_space=pltpu.SMEM)
STATS = [pltpu.VMEM((BLOCK, LANES), jnp.float32)] * 2


def assemble_call(meta, blocks):
    return pl.pallas_call(
        assemble,
        name="assemble",
        out_shape=[jax.ShapeDtypeStruct((GROUP_KEYS, 2 * HEAD), jnp.bfloat16)] * 2,
        in_specs=[SMEM] + [VMEM] * len(blocks),
        out_specs=[VMEM, VMEM],
        compiler_params=pltpu.CompilerParams(vmem_limit_bytes=12 << 20),
        cost_estimate=pl.CostEstimate(flops=1 << 20, transcendentals=0, bytes_accessed=3 << 20),
    )(meta, *blocks)


def cost(width):
    return pl.CostEstimate(
        flops=8 * BLOCK * GROUP_KEYS * width,
        transcendentals=BLOCK * GROUP_KEYS * width // HEAD,
        bytes_accessed=3 << 20,
    )


def visitor_call(d, meta, q, k, v):
    width = q.shape[1]
    return pl.pallas_call(
        functools.partial(attend_visitor, d),
        name=f"attend_{d}",
        out_shape=jax.ShapeDtypeStruct((BLOCK + 16, width), jnp.bfloat16),
        in_specs=[SMEM] + [VMEM] * 3,
        out_specs=VMEM,
        scratch_shapes=[pltpu.VMEM((BLOCK, GROUP_KEYS), jnp.bfloat16)] + STATS,
        compiler_params=pltpu.CompilerParams(vmem_limit_bytes=20 << 20),
        cost_estimate=cost(width),
    )(meta, q, k, v)


def own_call(meta, q, k, v, sink):
    width = q.shape[1]
    return pl.pallas_call(
        attend_own,
        name="attend_0",
        out_shape=jax.ShapeDtypeStruct((BLOCK + 16, width), jnp.float32),
        in_specs=[SMEM] + [VMEM] * 4,
        out_specs=VMEM,
        scratch_shapes=[pltpu.VMEM((BLOCK, 2 * HEAD), jnp.float32)] + STATS,
        compiler_params=pltpu.CompilerParams(vmem_limit_bytes=20 << 20),
        cost_estimate=cost(width),
    )(meta, q, k, v, sink)


def merge_call(meta, own, parts):
    return pl.pallas_call(
        merge,
        name="merge",
        out_shape=jax.ShapeDtypeStruct((BLOCK, own.shape[1]), jnp.bfloat16),
        in_specs=[SMEM] + [VMEM] * (1 + len(parts)),
        out_specs=VMEM,
        compiler_params=pltpu.CompilerParams(vmem_limit_bytes=16 << 20),
    )(meta, own, *parts)


def along_ring(x, step):
    return lax.ppermute(x, RING, [(i, (i + step) % N_RING) for i in range(N_RING)])


def to_group(x, step):
    return lax.ppermute(x, GROUP, [(i, i + step) for i in range(N_GROUPS) if 0 <= i + step < N_GROUPS])


def shards(queries, keys, values, doc_lengths):
    rows = queries.shape[0]
    kv_heads = keys.shape[1] // HEAD
    by_head = jnp.concatenate([x.reshape(rows, kv_heads, -1) for x in (queries, keys, values)], axis=2)
    mine = lax.all_to_all(by_head.reshape(rows, -1), "kvh", split_axis=1, concat_axis=0, tiled=True)
    width = queries.shape[1] // kv_heads
    q, kv = mine[:, :width], mine[:, width:]
    g, z = lax.axis_index(GROUP), lax.axis_index(RING)
    meta = jnp.concatenate([jnp.stack([g, z]).astype(jnp.int32), doc_lengths])

    half = BLOCK // 2
    visiting = {}
    blocks, up, down = [kv], kv, kv
    for step in range(3):
        up, down = along_ring(up, 1), along_ring(down, -1)
        visiting[REACH - step] = to_group(q, step - REACH)
        blocks += [up, down]
    blocks += [along_ring(up[:half], 1), along_ring(down[half:], -1)]
    visiting[1] = to_group(q, -1)

    first = blocks[0][:half]
    for r, i in enumerate((1, 3, 5, 7, 6, 4, 2), 1):
        first = jnp.where(z == r, blocks[i][:half], first)
    sink = jnp.zeros_like(first)
    for far in range(REACH + 1, N_GROUPS):
        got = lax.ppermute(first, GROUP, [(0, far)])
        sink = jnp.where(g == far, got, sink)

    k, v = assemble_call(meta, blocks)
    parts = []
    for d in range(REACH, 0, -1):
        parts.insert(0, to_group(visitor_call(d, meta, visiting[d], k, v), d))
    own = own_call(meta, q, k, v, sink)
    out = merge_call(meta, own, parts)
    return lax.all_to_all(out, "kvh", split_axis=0, concat_axis=1, tiled=True)


def solution(mesh):
    torus = Mesh(mesh.devices.reshape(2, 4, 8, mesh.shape["kvh"]), CTX_KVH)
    in_specs = (P(CTX_KVH, None), P(CTX_KVH, None), P(CTX_KVH, None), P())
    return jax.shard_map(
        shards, mesh=torus, in_specs=in_specs, out_specs=P(CTX_KVH, None), check_vma=False
    )
```

```python
import functools

import jax
import jax.numpy as jnp
from jax import lax
from jax.experimental import pallas as pl
from jax.experimental.pallas import tpu as pltpu
from jax.sharding import Mesh
from jax.sharding import PartitionSpec as P

HEAD = 128
SINK = 128
GROUP = ("ctx_0", "ctx_1")
RING = "ctx_2"
CTX_KVH = ("ctx_0", "ctx_1", "ctx_2", "kvh")
N_GROUPS, N_RING = 8, 8
REACH = 4
BLOCK = 256
GROUP_KEYS = N_RING * BLOCK
HALF = GROUP_KEYS // 2
UNROLL = 4
NEG = -1e30
LOG2E = 1.4426950408889634
SCALE = HEAD**-0.5 * LOG2E


LOW, HIGH, TINY = 2.0**-96, 2.0**96, 2.0**-120
LANES = 128
GATE = 24
NT = (((1,), (1,)), ((), ()))


def document_bounds(meta_ref):
    lane = lax.broadcasted_iota(jnp.int32, (1, LANES), 1)
    first, end = jnp.zeros((1, LANES), jnp.int32), jnp.zeros((1, LANES), jnp.int32)
    at = jnp.int32(0)
    for i in range(16):
        first = jnp.where(lane == i, at, first)
        at = at + meta_ref[2 + i]
        end = jnp.where(lane == i, at, end)
    return first, end


def start_of(meta_ref, pos):
    start, at = jnp.zeros_like(pos), jnp.int32(0)
    for i in range(15):
        at = at + meta_ref[2 + i]
        start = jnp.where(pos >= at, at, start)
    return start


def assemble(meta_ref, *refs):
    blocks, (k_ref, v_ref) = refs[:9], refs[9:]
    g, z = meta_ref[0], meta_ref[1]
    first, end = document_bounds(meta_ref)
    half = BLOCK // 2
    pieces = [(r, 0, ref) for ref, r in zip(blocks[:7], (0, 1, 7, 2, 6, 3, 5))]
    pieces += [(4, 0, blocks[7]), (4, half, blocks[8])]
    for r, offset, ref in pieces:
        n = ref.shape[0]
        block = lax.rem(z - r + N_RING, N_RING)
        at = pl.multiple_of(block * BLOCK + offset, half)
        rows = pl.ds(at, n)
        pos = g * GROUP_KEYS + at + lax.broadcasted_iota(jnp.int32, (n, 1), 0)
        seen = ((pos >= first) & (pos < end)) | (pos < SINK)
        k_ref[rows, :HEAD] = ref[:, :HEAD]
        k_ref[rows, HEAD:] = jnp.where(seen, 0.0, NEG).astype(k_ref.dtype)
        v_ref[rows, :HEAD] = ref[:, HEAD:]
        v_ref[rows, HEAD:] = jnp.ones((n, HEAD), v_ref.dtype)


def query_columns(meta_ref, q_first):
    first, end = document_bounds(meta_ref)
    pos = q_first + lax.broadcasted_iota(jnp.int32, (BLOCK, 1), 0)
    return jnp.where((pos >= first) & (pos < end), 1.0, 0.0).astype(jnp.bfloat16)


def scores(q, k):
    return lax.dot_general(q, k, NT, preferred_element_type=jnp.float32)


def finish(out_ref, stats_ref, h, o, m=None):
    total = o[:, HEAD:]
    cols = pl.ds(pl.multiple_of(h * HEAD, HEAD), HEAD)
    out_ref[:BLOCK, cols] = (o[:, :HEAD] / jnp.maximum(total, TINY)).astype(out_ref.dtype)
    lane = lax.broadcasted_iota(jnp.int32, total.shape, 1)
    stats = jnp.where(lane == h, total, stats_ref[...])
    stats_ref[...] = stats if m is None else jnp.where(lane == 8 + h, m, stats)


def put_stats(out_ref, rows, m):
    lse = (0.0 if m is None else m) + jnp.where(rows > 0.0, jnp.log2(jnp.maximum(rows, TINY)), NEG)
    words = []
    for _ in range(3):
        word = lse.astype(jnp.bfloat16).astype(jnp.float32)
        words.append(word)
        lse = lse - word
    lower = jnp.concatenate([words[0][:4], words[1][:4]], axis=0)
    out_ref[BLOCK:, :BLOCK] = jnp.concatenate([lower, words[2]], axis=0).astype(out_ref.dtype)
    out_ref[BLOCK:, BLOCK:] = jnp.zeros((16, out_ref.shape[1] - BLOCK), out_ref.dtype)


def weights_of(s, m=None):
    return jnp.exp2((s if m is None else s - m) * SCALE).astype(jnp.bfloat16)


def product(p, v):
    return jnp.dot(p, v, preferred_element_type=jnp.float32)


def attend(d, meta_ref, q_ref, k_ref, v_ref, *refs):
    own = d == 0
    sink_refs, (out_ref, acc_ref, p_ref, stats_ref, mask_ref) = refs[: int(own)], refs[int(own) :]
    heads = q_ref.shape[1] // HEAD
    g, z = meta_ref[0], meta_ref[1]
    q_first = (g + d) * GROUP_KEYS + z * BLOCK
    key_first, key_end = g * GROUP_KEYS, (g + 1) * GROUP_KEYS
    reach = start_of(meta_ref, q_first)
    far = g > REACH

    def query(h):
        return jnp.concatenate([q_ref[:, pl.ds(pl.multiple_of(h * HEAD, HEAD), HEAD)], mask_ref[...]], axis=1)

    def seen_scores(q, at):
        s = scores(q, k_ref[pl.ds(pl.multiple_of(at, BLOCK), BLOCK), :])
        if not own:
            return s
        row = lax.broadcasted_iota(jnp.int32, (BLOCK, BLOCK), 0)
        column = lax.broadcasted_iota(jnp.int32, (BLOCK, BLOCK), 1)
        return jnp.where(column - row <= z * BLOCK - at, s, NEG)

    def sink_scores(q):
        return scores(q[:, :HEAD], sink_refs[0][:, :HEAD])

    def sink_values():
        return jnp.concatenate([sink_refs[0][:, HEAD:], jnp.ones((SINK, HEAD), jnp.bfloat16)], axis=1)

    def each_head(body):
        lax.fori_loop(0, heads, lambda h, _: (body(h), 0)[1], 0)

    def store():
        stats_ref[...] = jnp.zeros((BLOCK, LANES), jnp.float32)
        for h in range(heads):
            finish(out_ref, stats_ref, h, acc_ref[h])
        totals = stats_ref[...].T[:8]
        put_stats(out_ref, totals, None)
        head = lax.broadcasted_iota(jnp.int32, totals.shape, 0)
        visible = head < heads
        if not own:
            pos = q_first + lax.broadcasted_iota(jnp.int32, totals.shape, 1)
            visible = visible & ((start_of(meta_ref, pos) < key_end) | (g == 0))
        off = visible & jnp.logical_not((totals >= LOW) & (totals <= HIGH))

        @pl.when(jnp.max(jnp.where(off, 1.0, 0.0)) > 0.0)
        def _():
            each_head(careful)
            rows = stats_ref[...].T
            put_stats(out_ref, rows[:8], rows[8:16])

    def careful(h):
        q = query(h)
        m = lax.fori_loop(
            0,
            N_RING,
            lambda r, m: jnp.maximum(m, jnp.max(seen_scores(q, r * BLOCK), axis=1, keepdims=True)),
            jnp.full((BLOCK, 1), 2 * NEG, jnp.float32),
        )
        if own:
            m = jnp.where(far, jnp.maximum(m, jnp.max(sink_scores(q), axis=1, keepdims=True)), m)

        def add(r, o):
            v = v_ref[pl.ds(pl.multiple_of(r * BLOCK, BLOCK), BLOCK), :]
            return o + product(weights_of(seen_scores(q, r * BLOCK), m), v)

        o = lax.fori_loop(0, N_RING, add, jnp.zeros((BLOCK, 2 * HEAD), jnp.float32))
        if own:
            o = o + jnp.where(far, product(weights_of(sink_scores(q), m), sink_values()), 0.0)
        finish(out_ref, stats_ref, h, o, m * SCALE)

    def over_halves():
        acc_ref[...] = jnp.zeros(acc_ref.shape, jnp.float32)
        low = ((reach >= key_first + HALF) & (g > 0)).astype(jnp.int32)
        high = 1 + (z * BLOCK >= HALF).astype(jnp.int32) if own else 2
        turns = heads // UNROLL

        def step(i, _):
            at = lax.div(i, turns) * HALF
            for u in range(UNROLL):
                h = lax.rem(i, turns) * UNROLL + u
                q = query(h)
                for r in range(0, HALF, BLOCK):
                    p_ref[u, :, r : r + BLOCK] = weights_of(seen_scores(q, at + r))
                acc_ref[h] += product(p_ref[u], v_ref[pl.ds(pl.multiple_of(at, HALF), HALF), :])
            return 0

        lax.fori_loop(low * turns, high * turns, step, 0)

    if own:
        mask_ref[...] = query_columns(meta_ref, q_first)
        over_halves()

        @pl.when(far)
        def _():
            def add_sink(h):
                acc_ref[h] += product(weights_of(sink_scores(query(h))), sink_values())

            each_head(add_sink)

        store()
        return
    near = reach < key_end
    active = (g + d < N_GROUPS) & (near | (g == 0))

    @pl.when(active)
    def _():
        mask_ref[...] = query_columns(meta_ref, q_first)
        pl.when(near)(over_halves)

        @pl.when(jnp.logical_not(near))
        def _():
            def only_sink(h):
                acc_ref[h] = product(weights_of(seen_scores(query(h), 0)), v_ref[:BLOCK, :])

            each_head(only_sink)

        store()

    @pl.when(jnp.logical_not(active))
    def _():
        out_ref[:BLOCK, :] = jnp.zeros((BLOCK, q_ref.shape[1]), out_ref.dtype)
        out_ref[BLOCK:, :] = jnp.full((16, q_ref.shape[1]), NEG, out_ref.dtype)


def merge(meta_ref, own_ref, *refs):
    parts, out_ref = refs[:REACH], refs[REACH]
    g = meta_ref[0]
    heads = out_ref.shape[1] // HEAD

    def lse_of(ref):
        words = ref[BLOCK:, :BLOCK].astype(jnp.float32)
        return words[0:4] + words[4:8] + words[8:12]

    lses = [lse_of(own_ref)] + [jnp.where(g >= d, lse_of(ref), NEG) for d, ref in enumerate(parts, 1)]
    top = functools.reduce(jnp.maximum, lses)
    weights = [jnp.exp2(x - top) for x in lses]
    total = functools.reduce(jnp.add, weights)
    rows = [w / total for w in weights]
    rows.append(jnp.zeros((LANES - heads * (REACH + 1), BLOCK), jnp.float32))
    columns = jnp.concatenate(rows, axis=0).T
    for h in range(heads):
        cols = slice(h * HEAD, (h + 1) * HEAD)
        acc = own_ref[:BLOCK, cols] * columns[:, h : h + 1]
        for d, ref in enumerate(parts, 1):
            acc = acc + ref[:BLOCK, cols].astype(jnp.float32) * columns[:, heads * d + h : heads * d + h + 1]
        out_ref[:, cols] = acc.astype(out_ref.dtype)


VMEM = pl.BlockSpec(memory_space=pltpu.VMEM)
SMEM = pl.BlockSpec(memory_space=pltpu.SMEM)


def assemble_call(meta, blocks):
    return pl.pallas_call(
        assemble,
        name="assemble",
        out_shape=[jax.ShapeDtypeStruct((GROUP_KEYS, 2 * HEAD), jnp.bfloat16)] * 2,
        in_specs=[SMEM] + [VMEM] * len(blocks),
        out_specs=[VMEM, VMEM],
        compiler_params=pltpu.CompilerParams(vmem_limit_bytes=12 << 20),
        cost_estimate=pl.CostEstimate(flops=1 << 20, transcendentals=0, bytes_accessed=3 << 20),
    )(meta, *blocks)


def cost(width):
    return pl.CostEstimate(flops=2 * BLOCK * GROUP_KEYS * width, transcendentals=0, bytes_accessed=3 << 20)


def attend_call(d, meta, q, k, v, *sink):
    width = q.shape[1]
    return pl.pallas_call(
        functools.partial(attend, d),
        name=f"attend_{d}",
        out_shape=jax.ShapeDtypeStruct((BLOCK + 16, width), jnp.bfloat16 if d else jnp.float32),
        in_specs=[SMEM] + [VMEM] * (3 + len(sink)),
        out_specs=VMEM,
        scratch_shapes=[
            pltpu.VMEM((width // HEAD, BLOCK, 2 * HEAD), jnp.float32),
            pltpu.VMEM((UNROLL, BLOCK, HALF), jnp.bfloat16),
            pltpu.VMEM((BLOCK, LANES), jnp.float32),
            pltpu.VMEM((BLOCK, LANES), jnp.bfloat16),
        ],
        compiler_params=pltpu.CompilerParams(vmem_limit_bytes=20 << 20),
        cost_estimate=cost(width),
    )(meta, q, k, v, *sink)


def merge_call(meta, own, parts):
    return pl.pallas_call(
        merge,
        name="merge",
        out_shape=jax.ShapeDtypeStruct((BLOCK, own.shape[1]), jnp.bfloat16),
        in_specs=[SMEM] + [VMEM] * (1 + len(parts)),
        out_specs=VMEM,
        compiler_params=pltpu.CompilerParams(vmem_limit_bytes=16 << 20),
    )(meta, own, *parts)


def along_ring(x, step):
    return lax.ppermute(x, RING, [(i, (i + step) % N_RING) for i in range(N_RING)])


def to_group(x, step):
    return lax.ppermute(x, GROUP, [(i, i + step) for i in range(N_GROUPS) if 0 <= i + step < N_GROUPS])


def shards(queries, keys, values, doc_lengths):
    rows = queries.shape[0]
    kv_heads = keys.shape[1] // HEAD
    by_head = jnp.concatenate([x.reshape(rows, kv_heads, -1) for x in (queries, keys, values)], axis=2)
    mine = lax.all_to_all(by_head.reshape(rows, -1), "kvh", split_axis=1, concat_axis=0, tiled=True)
    width = queries.shape[1] // kv_heads
    q, kv = mine[:, :width], mine[:, width:]
    g, z = lax.axis_index(GROUP), lax.axis_index(RING)
    meta = jnp.concatenate([jnp.stack([g, z]).astype(jnp.int32), doc_lengths])

    half = BLOCK // 2
    visiting = {}
    blocks, up, down = [kv], kv, kv
    for step in range(3):
        up, down = along_ring(up, 1), along_ring(down, -1)
        visiting[REACH - step] = to_group(q, step - REACH)
        blocks += [up, down]
    blocks += [along_ring(up[:half], 1), along_ring(down[half:], -1)]
    visiting[1] = to_group(q, -1)

    k, v = assemble_call(meta, blocks)
    parts = {}
    first = blocks[0][:half]
    for r, i in enumerate((1, 3, 5, 7, 6, 4, 2), 1):
        first = jnp.where(z == r, blocks[i][:half], first)
    order = (1, 2, 3, 4)
    for turn, d in enumerate(order):
        part = attend_call(d, meta, visiting[d], k, v)
        if turn == 1:
            part, first = lax.optimization_barrier((part, first))
            sink = jnp.zeros_like(first)
            for far in range(REACH + 1, N_GROUPS):
                sink = jnp.where(g == far, lax.ppermute(first, GROUP, [(0, far)]), sink)
        parts[d] = to_group(part, d)
    own = attend_call(0, meta, q, k, v, sink)
    parts = [parts[d] for d in range(1, REACH + 1)]
    out = merge_call(meta, own, parts)
    return lax.all_to_all(out, "kvh", split_axis=0, concat_axis=1, tiled=True)


def solution(mesh):
    torus = Mesh(mesh.devices.reshape(2, 4, 8, mesh.shape["kvh"]), CTX_KVH)
    in_specs = (P(CTX_KVH, None), P(CTX_KVH, None), P(CTX_KVH, None), P())
    return jax.shard_map(
        shards, mesh=torus, in_specs=in_specs, out_specs=P(CTX_KVH, None), check_vma=False
    )
```

```python
import functools

import jax
import jax.numpy as jnp
from jax import lax
from jax.experimental import pallas as pl
from jax.experimental.pallas import tpu as pltpu
from jax.sharding import Mesh
from jax.sharding import PartitionSpec as P

HEAD = 128
SINK = 128
GROUP = ("ctx_0", "ctx_1")
RING = "ctx_2"
CTX_KVH = ("ctx_0", "ctx_1", "ctx_2", "kvh")
N_GROUPS, N_RING = 8, 8
REACH = 4
BLOCK = 256
GROUP_KEYS = N_RING * BLOCK
HALF = GROUP_KEYS // 2
UNROLL = 4
NEG = -1e30
LOG2E = 1.4426950408889634
SCALE = HEAD**-0.5 * LOG2E


LOW, HIGH, TINY = 2.0**-96, 2.0**96, 2.0**-120
LANES = 128
GATE = 24
NT = (((1,), (1,)), ((), ()))


def document_bounds(meta_ref):
    lane = lax.broadcasted_iota(jnp.int32, (1, LANES), 1)
    first, end = jnp.zeros((1, LANES), jnp.int32), jnp.zeros((1, LANES), jnp.int32)
    at = jnp.int32(0)
    for i in range(16):
        first = jnp.where(lane == i, at, first)
        at = at + meta_ref[2 + i]
        end = jnp.where(lane == i, at, end)
    return first, end


def start_of(meta_ref, pos):
    start, at = jnp.zeros_like(pos), jnp.int32(0)
    for i in range(15):
        at = at + meta_ref[2 + i]
        start = jnp.where(pos >= at, at, start)
    return start


def assemble(meta_ref, *refs):
    blocks, (k_ref, v_ref) = refs[:8], refs[8:]
    g, z = meta_ref[0], meta_ref[1]
    first, end = document_bounds(meta_ref)
    pieces = list(zip((0, 1, 7, 2, 6, 3, 5, 4), blocks))
    for r, ref in pieces:
        n = ref.shape[0]
        block = lax.rem(z - r + N_RING, N_RING)
        at = pl.multiple_of(block * BLOCK, BLOCK)
        rows = pl.ds(at, n)
        pos = g * GROUP_KEYS + at + lax.broadcasted_iota(jnp.int32, (n, 1), 0)
        seen = ((pos >= first) & (pos < end)) | (pos < SINK)
        k_ref[rows, :HEAD] = ref[:, :HEAD]
        k_ref[rows, HEAD:] = jnp.where(seen, 0.0, NEG).astype(k_ref.dtype)
        v_ref[rows, :HEAD] = ref[:, HEAD:]
        v_ref[rows, HEAD:] = jnp.ones((n, HEAD), v_ref.dtype)


def query_columns(meta_ref, q_first):
    first, end = document_bounds(meta_ref)
    pos = q_first + lax.broadcasted_iota(jnp.int32, (BLOCK, 1), 0)
    return jnp.where((pos >= first) & (pos < end), 1.0, 0.0).astype(jnp.bfloat16)


def scores(q, k):
    return lax.dot_general(q, k, NT, preferred_element_type=jnp.float32)


def finish(out_ref, stats_ref, h, o, m=None):
    total = o[:, HEAD:]
    cols = pl.ds(pl.multiple_of(h * HEAD, HEAD), HEAD)
    out_ref[:BLOCK, cols] = (o[:, :HEAD] / jnp.maximum(total, TINY)).astype(out_ref.dtype)
    lane = lax.broadcasted_iota(jnp.int32, total.shape, 1)
    stats = jnp.where(lane == h, total, stats_ref[...])
    stats_ref[...] = stats if m is None else jnp.where(lane == 8 + h, m, stats)


def put_stats(out_ref, rows, m):
    lse = (0.0 if m is None else m) + jnp.where(rows > 0.0, jnp.log2(jnp.maximum(rows, TINY)), NEG)
    words = []
    for _ in range(3):
        word = lse.astype(jnp.bfloat16).astype(jnp.float32)
        words.append(word)
        lse = lse - word
    lower = jnp.concatenate([words[0][:4], words[1][:4]], axis=0)
    out_ref[BLOCK:, :BLOCK] = jnp.concatenate([lower, words[2]], axis=0).astype(out_ref.dtype)
    out_ref[BLOCK:, BLOCK:] = jnp.zeros((16, out_ref.shape[1] - BLOCK), out_ref.dtype)


def weights_of(s, m=None):
    return jnp.exp2((s if m is None else s - m) * SCALE).astype(jnp.bfloat16)


def product(p, v):
    return jnp.dot(p, v, preferred_element_type=jnp.float32)


def attend(d, meta_ref, q_ref, k_ref, v_ref, *refs):
    own = d == 0
    sink_refs, (out_ref, acc_ref, p_ref, stats_ref, mask_ref) = refs[: int(own)], refs[int(own) :]
    heads = q_ref.shape[1] // HEAD
    g, z = meta_ref[0], meta_ref[1]
    q_first = (g + d) * GROUP_KEYS + z * BLOCK
    key_first, key_end = g * GROUP_KEYS, (g + 1) * GROUP_KEYS
    reach = start_of(meta_ref, q_first)
    far = g > REACH

    def query(h):
        return jnp.concatenate([q_ref[:, pl.ds(pl.multiple_of(h * HEAD, HEAD), HEAD)], mask_ref[...]], axis=1)

    def seen_scores(q, at):
        s = scores(q, k_ref[pl.ds(pl.multiple_of(at, BLOCK), BLOCK), :])
        if not own:
            return s
        row = lax.broadcasted_iota(jnp.int32, (BLOCK, BLOCK), 0)
        column = lax.broadcasted_iota(jnp.int32, (BLOCK, BLOCK), 1)
        return jnp.where(column - row <= z * BLOCK - at, s, NEG)

    def sink_scores(q):
        return scores(q[:, :HEAD], sink_refs[0][:, :HEAD])

    def sink_values():
        return jnp.concatenate([sink_refs[0][:, HEAD:], jnp.ones((SINK, HEAD), jnp.bfloat16)], axis=1)

    def each_head(body):
        lax.fori_loop(0, heads, lambda h, _: (body(h), 0)[1], 0)

    def store():
        stats_ref[...] = jnp.zeros((BLOCK, LANES), jnp.float32)
        for h in range(heads):
            finish(out_ref, stats_ref, h, acc_ref[h])
        totals = stats_ref[...].T[:8]
        put_stats(out_ref, totals, None)
        head = lax.broadcasted_iota(jnp.int32, totals.shape, 0)
        visible = head < heads
        if not own:
            pos = q_first + lax.broadcasted_iota(jnp.int32, totals.shape, 1)
            visible = visible & ((start_of(meta_ref, pos) < key_end) | (g == 0))
        off = visible & jnp.logical_not((totals >= LOW) & (totals <= HIGH))

        @pl.when(jnp.max(jnp.where(off, 1.0, 0.0)) > 0.0)
        def _():
            each_head(careful)
            rows = stats_ref[...].T
            put_stats(out_ref, rows[:8], rows[8:16])

    def careful(h):
        q = query(h)
        m = lax.fori_loop(
            0,
            N_RING,
            lambda r, m: jnp.maximum(m, jnp.max(seen_scores(q, r * BLOCK), axis=1, keepdims=True)),
            jnp.full((BLOCK, 1), 2 * NEG, jnp.float32),
        )
        if own:
            m = jnp.where(far, jnp.maximum(m, jnp.max(sink_scores(q), axis=1, keepdims=True)), m)

        def add(r, o):
            v = v_ref[pl.ds(pl.multiple_of(r * BLOCK, BLOCK), BLOCK), :]
            return o + product(weights_of(seen_scores(q, r * BLOCK), m), v)

        o = lax.fori_loop(0, N_RING, add, jnp.zeros((BLOCK, 2 * HEAD), jnp.float32))
        if own:
            o = o + jnp.where(far, product(weights_of(sink_scores(q), m), sink_values()), 0.0)
        finish(out_ref, stats_ref, h, o, m * SCALE)

    def over_halves():
        acc_ref[...] = jnp.zeros(acc_ref.shape, jnp.float32)
        low = ((reach >= key_first + HALF) & (g > 0)).astype(jnp.int32)
        high = 1 + (z * BLOCK >= HALF).astype(jnp.int32) if own else 2
        turns = heads // UNROLL

        def step(i, _):
            at = lax.div(i, turns) * HALF
            for u in range(UNROLL):
                h = lax.rem(i, turns) * UNROLL + u
                q = query(h)
                for r in range(0, HALF, BLOCK):
                    p_ref[u, :, r : r + BLOCK] = weights_of(seen_scores(q, at + r))
                acc_ref[h] += product(p_ref[u], v_ref[pl.ds(pl.multiple_of(at, HALF), HALF), :])
            return 0

        lax.fori_loop(low * turns, high * turns, step, 0)

    if own:
        mask_ref[...] = query_columns(meta_ref, q_first)
        over_halves()

        @pl.when(far)
        def _():
            def add_sink(h):
                acc_ref[h] += product(weights_of(sink_scores(query(h))), sink_values())

            each_head(add_sink)

        store()
        return
    near = reach < key_end
    active = (g + d < N_GROUPS) & (near | (g == 0))

    @pl.when(active)
    def _():
        mask_ref[...] = query_columns(meta_ref, q_first)
        pl.when(near)(over_halves)

        @pl.when(jnp.logical_not(near))
        def _():
            def only_sink(h):
                acc_ref[h] = product(weights_of(seen_scores(query(h), 0)), v_ref[:BLOCK, :])

            each_head(only_sink)

        store()

    @pl.when(jnp.logical_not(active))
    def _():
        out_ref[:BLOCK, :] = jnp.zeros((BLOCK, q_ref.shape[1]), out_ref.dtype)
        out_ref[BLOCK:, :] = jnp.full((16, q_ref.shape[1]), NEG, out_ref.dtype)


def merge(meta_ref, own_ref, *refs):
    parts, out_ref = refs[:REACH], refs[REACH]
    g = meta_ref[0]
    heads = out_ref.shape[1] // HEAD

    def lse_of(ref):
        words = ref[BLOCK:, :BLOCK].astype(jnp.float32)
        return words[0:4] + words[4:8] + words[8:12]

    lses = [lse_of(own_ref)] + [jnp.where(g >= d, lse_of(ref), NEG) for d, ref in enumerate(parts, 1)]
    top = functools.reduce(jnp.maximum, lses)
    weights = [jnp.exp2(x - top) for x in lses]
    total = functools.reduce(jnp.add, weights)
    rows = [w / total for w in weights]
    rows.append(jnp.zeros((LANES - heads * (REACH + 1), BLOCK), jnp.float32))
    columns = jnp.concatenate(rows, axis=0).T
    for h in range(heads):
        cols = slice(h * HEAD, (h + 1) * HEAD)
        acc = own_ref[:BLOCK, cols] * columns[:, h : h + 1]
        for d, ref in enumerate(parts, 1):
            acc = acc + ref[:BLOCK, cols].astype(jnp.float32) * columns[:, heads * d + h : heads * d + h + 1]
        out_ref[:, cols] = acc.astype(out_ref.dtype)


VMEM = pl.BlockSpec(memory_space=pltpu.VMEM)
SMEM = pl.BlockSpec(memory_space=pltpu.SMEM)


def assemble_call(meta, blocks):
    return pl.pallas_call(
        assemble,
        name="assemble",
        out_shape=[jax.ShapeDtypeStruct((GROUP_KEYS, 2 * HEAD), jnp.bfloat16)] * 2,
        in_specs=[SMEM] + [VMEM] * len(blocks),
        out_specs=[VMEM, VMEM],
        compiler_params=pltpu.CompilerParams(vmem_limit_bytes=12 << 20),
        cost_estimate=pl.CostEstimate(flops=1 << 20, transcendentals=0, bytes_accessed=3 << 20),
    )(meta, *blocks)


def cost(width):
    return pl.CostEstimate(flops=2 * BLOCK * GROUP_KEYS * width, transcendentals=0, bytes_accessed=3 << 20)


def attend_call(d, meta, q, k, v, *sink):
    width = q.shape[1]
    return pl.pallas_call(
        functools.partial(attend, d),
        name=f"attend_{d}",
        out_shape=jax.ShapeDtypeStruct((BLOCK + 16, width), jnp.bfloat16 if d else jnp.float32),
        in_specs=[SMEM] + [VMEM] * (3 + len(sink)),
        out_specs=VMEM,
        scratch_shapes=[
            pltpu.VMEM((width // HEAD, BLOCK, 2 * HEAD), jnp.float32),
            pltpu.VMEM((UNROLL, BLOCK, HALF), jnp.bfloat16),
            pltpu.VMEM((BLOCK, LANES), jnp.float32),
            pltpu.VMEM((BLOCK, LANES), jnp.bfloat16),
        ],
        compiler_params=pltpu.CompilerParams(vmem_limit_bytes=20 << 20),
        cost_estimate=cost(width),
    )(meta, q, k, v, *sink)


def merge_call(meta, own, parts):
    return pl.pallas_call(
        merge,
        name="merge",
        out_shape=jax.ShapeDtypeStruct((BLOCK, own.shape[1]), jnp.bfloat16),
        in_specs=[SMEM] + [VMEM] * (1 + len(parts)),
        out_specs=VMEM,
        compiler_params=pltpu.CompilerParams(vmem_limit_bytes=16 << 20),
    )(meta, own, *parts)


def along_ring(x, step):
    return lax.ppermute(x, RING, [(i, (i + step) % N_RING) for i in range(N_RING)])


def to_group(x, step):
    return lax.ppermute(x, GROUP, [(i, i + step) for i in range(N_GROUPS) if 0 <= i + step < N_GROUPS])


def shards(queries, keys, values, doc_lengths):
    rows = queries.shape[0]
    kv_heads = keys.shape[1] // HEAD
    by_head = jnp.concatenate([x.reshape(rows, kv_heads, -1) for x in (queries, keys, values)], axis=2)
    mine = lax.all_to_all(by_head.reshape(rows, -1), "kvh", split_axis=1, concat_axis=0, tiled=True)
    width = queries.shape[1] // kv_heads
    q, kv = mine[:, :width], mine[:, width:]
    g, z = lax.axis_index(GROUP), lax.axis_index(RING)
    meta = jnp.concatenate([jnp.stack([g, z]).astype(jnp.int32), doc_lengths])

    half = BLOCK // 2
    visiting = {}
    blocks, up, down = [kv], kv, kv
    for step in range(3):
        up, down = along_ring(up, 1), along_ring(down, -1)
        blocks += [up, down]
    blocks.append(along_ring(up, 1))
    for d in range(1, REACH + 1):
        visiting[d] = to_group(q, -d)
    k, v = assemble_call(meta, blocks)
    parts = {}
    first = blocks[0][:half]
    for r, i in enumerate((1, 3, 5, 7, 6, 4, 2), 1):
        first = jnp.where(z == r, blocks[i][:half], first)
    order = (1, 2, 3, 4)
    for turn, d in enumerate(order):
        part = attend_call(d, meta, visiting[d], k, v)
        if turn == 1:
            part, first = lax.optimization_barrier((part, first))
            sink = jnp.zeros_like(first)
            for far in range(REACH + 1, N_GROUPS):
                sink = jnp.where(g == far, lax.ppermute(first, GROUP, [(0, far)]), sink)
        parts[d] = to_group(part, d)
    own = attend_call(0, meta, q, k, v, sink)
    parts = [parts[d] for d in range(1, REACH + 1)]
    out = merge_call(meta, own, parts)
    return lax.all_to_all(out, "kvh", split_axis=0, concat_axis=1, tiled=True)


def solution(mesh):
    torus = Mesh(mesh.devices.reshape(2, 4, 8, mesh.shape["kvh"]), CTX_KVH)
    in_specs = (P(CTX_KVH, None), P(CTX_KVH, None), P(CTX_KVH, None), P())
    return jax.shard_map(
        shards, mesh=torus, in_specs=in_specs, out_specs=P(CTX_KVH, None), check_vma=False
    )
```

```python
import functools

import jax
import jax.numpy as jnp
from jax import lax
from jax.experimental import pallas as pl
from jax.experimental.pallas import tpu as pltpu
from jax.sharding import Mesh
from jax.sharding import PartitionSpec as P

HEAD = 128
SINK = 128
GROUP = ("ctx_0", "ctx_1")
RING = "ctx_2"
CTX_KVH = ("ctx_0", "ctx_1", "ctx_2", "kvh")
N_GROUPS, N_RING = 8, 8
REACH = 4
BLOCK = 256
GROUP_KEYS = N_RING * BLOCK
HALF = GROUP_KEYS // 2
UNROLL = 4
NEG = -1e30
LOG2E = 1.4426950408889634
SCALE = HEAD**-0.5 * LOG2E


LOW, HIGH, TINY = 2.0**-96, 2.0**96, 2.0**-120
LANES = 128
GATE = 24
NT = (((1,), (1,)), ((), ()))


def document_bounds(meta_ref):
    lane = lax.broadcasted_iota(jnp.int32, (1, LANES), 1)
    first, end = jnp.zeros((1, LANES), jnp.int32), jnp.zeros((1, LANES), jnp.int32)
    at = jnp.int32(0)
    for i in range(16):
        first = jnp.where(lane == i, at, first)
        at = at + meta_ref[2 + i]
        end = jnp.where(lane == i, at, end)
    return first, end


def start_of(meta_ref, pos):
    start, at = jnp.zeros_like(pos), jnp.int32(0)
    for i in range(15):
        at = at + meta_ref[2 + i]
        start = jnp.where(pos >= at, at, start)
    return start


def assemble(places, meta_ref, *refs):
    blocks, (k_ref, v_ref) = refs[: len(places)], refs[-2:]
    g, z = meta_ref[0], meta_ref[1]
    first, end = document_bounds(meta_ref)
    pieces = list(zip(places, blocks))
    for r, ref in pieces:
        n = ref.shape[0]
        block = lax.rem(z - r + N_RING, N_RING)
        at = pl.multiple_of(block * BLOCK, BLOCK)
        rows = pl.ds(at, n)
        pos = g * GROUP_KEYS + at + lax.broadcasted_iota(jnp.int32, (n, 1), 0)
        seen = ((pos >= first) & (pos < end)) | (pos < SINK)
        k_ref[rows, :HEAD] = ref[:, :HEAD]
        k_ref[rows, HEAD:] = jnp.where(seen, 0.0, NEG).astype(k_ref.dtype)
        v_ref[rows, :HEAD] = ref[:, HEAD:]
        v_ref[rows, HEAD:] = jnp.ones((n, HEAD), v_ref.dtype)


def query_columns(meta_ref, q_first):
    first, end = document_bounds(meta_ref)
    pos = q_first + lax.broadcasted_iota(jnp.int32, (BLOCK, 1), 0)
    return jnp.where((pos >= first) & (pos < end), 1.0, 0.0).astype(jnp.bfloat16)


def scores(q, k):
    return lax.dot_general(q, k, NT, preferred_element_type=jnp.float32)


def finish(out_ref, stats_ref, h, o, m=None):
    total = o[:, HEAD:]
    cols = pl.ds(pl.multiple_of(h * HEAD, HEAD), HEAD)
    out_ref[:BLOCK, cols] = (o[:, :HEAD] / jnp.maximum(total, TINY)).astype(out_ref.dtype)
    lane = lax.broadcasted_iota(jnp.int32, total.shape, 1)
    stats = jnp.where(lane == h, total, stats_ref[...])
    stats_ref[...] = stats if m is None else jnp.where(lane == 8 + h, m, stats)


def put_stats(out_ref, rows, m):
    lse = (0.0 if m is None else m) + jnp.where(rows > 0.0, jnp.log2(jnp.maximum(rows, TINY)), NEG)
    words = []
    for _ in range(3):
        word = lse.astype(jnp.bfloat16).astype(jnp.float32)
        words.append(word)
        lse = lse - word
    lower = jnp.concatenate([words[0][:4], words[1][:4]], axis=0)
    out_ref[BLOCK:, :BLOCK] = jnp.concatenate([lower, words[2]], axis=0).astype(out_ref.dtype)
    out_ref[BLOCK:, BLOCK:] = jnp.zeros((16, out_ref.shape[1] - BLOCK), out_ref.dtype)


def weights_of(s, m=None):
    return jnp.exp2((s if m is None else s - m) * SCALE).astype(jnp.bfloat16)


def product(p, v):
    return jnp.dot(p, v, preferred_element_type=jnp.float32)


def attend(d, meta_ref, q_ref, k_ref, v_ref, *refs):
    own = d == 0
    sink_refs, (out_ref, acc_ref, p_ref, stats_ref, mask_ref) = refs[: int(own)], refs[int(own) :]
    heads = q_ref.shape[1] // HEAD
    g, z = meta_ref[0], meta_ref[1]
    q_first = (g + d) * GROUP_KEYS + z * BLOCK
    key_first, key_end = g * GROUP_KEYS, (g + 1) * GROUP_KEYS
    reach = start_of(meta_ref, q_first)
    far = g > REACH

    def query(h):
        return jnp.concatenate([q_ref[:, pl.ds(pl.multiple_of(h * HEAD, HEAD), HEAD)], mask_ref[...]], axis=1)

    def seen_scores(q, at):
        s = scores(q, k_ref[pl.ds(pl.multiple_of(at, BLOCK), BLOCK), :])
        if not own:
            return s
        row = lax.broadcasted_iota(jnp.int32, (BLOCK, BLOCK), 0)
        column = lax.broadcasted_iota(jnp.int32, (BLOCK, BLOCK), 1)
        return jnp.where(column - row <= z * BLOCK - at, s, NEG)

    def sink_scores(q):
        return scores(q[:, :HEAD], sink_refs[0][:, :HEAD])

    def sink_values():
        return jnp.concatenate([sink_refs[0][:, HEAD:], jnp.ones((SINK, HEAD), jnp.bfloat16)], axis=1)

    def each_head(body):
        lax.fori_loop(0, heads, lambda h, _: (body(h), 0)[1], 0)

    def store():
        stats_ref[...] = jnp.zeros((BLOCK, LANES), jnp.float32)
        for h in range(heads):
            finish(out_ref, stats_ref, h, acc_ref[h])
        totals = stats_ref[...].T[:8]
        put_stats(out_ref, totals, None)
        head = lax.broadcasted_iota(jnp.int32, totals.shape, 0)
        visible = head < heads
        if not own:
            pos = q_first + lax.broadcasted_iota(jnp.int32, totals.shape, 1)
            visible = visible & ((start_of(meta_ref, pos) < key_end) | (g == 0))
        off = visible & jnp.logical_not((totals >= LOW) & (totals <= HIGH))

        @pl.when(jnp.max(jnp.where(off, 1.0, 0.0)) > 0.0)
        def _():
            each_head(careful)
            rows = stats_ref[...].T
            put_stats(out_ref, rows[:8], rows[8:16])

    def careful(h):
        q = query(h)
        m = lax.fori_loop(
            0,
            N_RING,
            lambda r, m: jnp.maximum(m, jnp.max(seen_scores(q, r * BLOCK), axis=1, keepdims=True)),
            jnp.full((BLOCK, 1), 2 * NEG, jnp.float32),
        )
        if own:
            m = jnp.where(far, jnp.maximum(m, jnp.max(sink_scores(q), axis=1, keepdims=True)), m)

        def add(r, o):
            v = v_ref[pl.ds(pl.multiple_of(r * BLOCK, BLOCK), BLOCK), :]
            return o + product(weights_of(seen_scores(q, r * BLOCK), m), v)

        o = lax.fori_loop(0, N_RING, add, jnp.zeros((BLOCK, 2 * HEAD), jnp.float32))
        if own:
            o = o + jnp.where(far, product(weights_of(sink_scores(q), m), sink_values()), 0.0)
        finish(out_ref, stats_ref, h, o, m * SCALE)

    def over_halves():
        acc_ref[...] = jnp.zeros(acc_ref.shape, jnp.float32)
        low = ((reach >= key_first + HALF) & (g > 0)).astype(jnp.int32)
        high = 1 + (z * BLOCK >= HALF).astype(jnp.int32) if own else 2
        turns = heads // UNROLL

        def step(i, _):
            at = lax.div(i, turns) * HALF
            for u in range(UNROLL):
                h = lax.rem(i, turns) * UNROLL + u
                q = query(h)
                for r in range(0, HALF, BLOCK):
                    p_ref[u, :, r : r + BLOCK] = weights_of(seen_scores(q, at + r))
                acc_ref[h] += product(p_ref[u], v_ref[pl.ds(pl.multiple_of(at, HALF), HALF), :])
            return 0

        lax.fori_loop(low * turns, high * turns, step, 0)

    if own:
        mask_ref[...] = query_columns(meta_ref, q_first)
        over_halves()

        @pl.when(far)
        def _():
            def add_sink(h):
                acc_ref[h] += product(weights_of(sink_scores(query(h))), sink_values())

            each_head(add_sink)

        store()
        return
    near = reach < key_end
    active = (g + d < N_GROUPS) & (near | (g == 0))

    @pl.when(active)
    def _():
        mask_ref[...] = query_columns(meta_ref, q_first)
        pl.when(near)(over_halves)

        @pl.when(jnp.logical_not(near))
        def _():
            def only_sink(h):
                acc_ref[h] = product(weights_of(seen_scores(query(h), 0)), v_ref[:BLOCK, :])

            each_head(only_sink)

        store()

    @pl.when(jnp.logical_not(active))
    def _():
        out_ref[:BLOCK, :] = jnp.zeros((BLOCK, q_ref.shape[1]), out_ref.dtype)
        out_ref[BLOCK:, :] = jnp.full((16, q_ref.shape[1]), NEG, out_ref.dtype)


def merge(meta_ref, own_ref, *refs):
    parts, out_ref = refs[:REACH], refs[REACH]
    g = meta_ref[0]
    heads = out_ref.shape[1] // HEAD

    def lse_of(ref):
        words = ref[BLOCK:, :BLOCK].astype(jnp.float32)
        return words[0:4] + words[4:8] + words[8:12]

    lses = [lse_of(own_ref)] + [jnp.where(g >= d, lse_of(ref), NEG) for d, ref in enumerate(parts, 1)]
    top = functools.reduce(jnp.maximum, lses)
    weights = [jnp.exp2(x - top) for x in lses]
    total = functools.reduce(jnp.add, weights)
    rows = [w / total for w in weights]
    rows.append(jnp.zeros((LANES - heads * (REACH + 1), BLOCK), jnp.float32))
    columns = jnp.concatenate(rows, axis=0).T
    for h in range(heads):
        cols = slice(h * HEAD, (h + 1) * HEAD)
        acc = own_ref[:BLOCK, cols] * columns[:, h : h + 1]
        for d, ref in enumerate(parts, 1):
            acc = acc + ref[:BLOCK, cols].astype(jnp.float32) * columns[:, heads * d + h : heads * d + h + 1]
        out_ref[:, cols] = acc.astype(out_ref.dtype)


VMEM = pl.BlockSpec(memory_space=pltpu.VMEM)
SMEM = pl.BlockSpec(memory_space=pltpu.SMEM)


def assemble_call(meta, places, blocks, *held):
    n = 1 + len(blocks)
    return pl.pallas_call(
        functools.partial(assemble, places),
        name=f"assemble_{len(places)}",
        out_shape=[jax.ShapeDtypeStruct((GROUP_KEYS, 2 * HEAD), jnp.bfloat16)] * 2,
        in_specs=[SMEM] + [VMEM] * (len(blocks) + len(held)),
        out_specs=[VMEM, VMEM],
        input_output_aliases={n: 0, n + 1: 1} if held else {},
        compiler_params=pltpu.CompilerParams(vmem_limit_bytes=12 << 20),
        cost_estimate=pl.CostEstimate(flops=1 << 20, transcendentals=0, bytes_accessed=3 << 20),
    )(meta, *blocks, *held)


def cost(width):
    return pl.CostEstimate(flops=2 * BLOCK * GROUP_KEYS * width, transcendentals=0, bytes_accessed=3 << 20)


def attend_call(d, meta, q, k, v, *sink):
    width = q.shape[1]
    return pl.pallas_call(
        functools.partial(attend, d),
        name=f"attend_{d}",
        out_shape=jax.ShapeDtypeStruct((BLOCK + 16, width), jnp.bfloat16 if d else jnp.float32),
        in_specs=[SMEM] + [VMEM] * (3 + len(sink)),
        out_specs=VMEM,
        scratch_shapes=[
            pltpu.VMEM((width // HEAD, BLOCK, 2 * HEAD), jnp.float32),
            pltpu.VMEM((UNROLL, BLOCK, HALF), jnp.bfloat16),
            pltpu.VMEM((BLOCK, LANES), jnp.float32),
            pltpu.VMEM((BLOCK, LANES), jnp.bfloat16),
        ],
        compiler_params=pltpu.CompilerParams(vmem_limit_bytes=20 << 20),
        cost_estimate=cost(width),
    )(meta, q, k, v, *sink)


def merge_call(meta, own, parts):
    return pl.pallas_call(
        merge,
        name="merge",
        out_shape=jax.ShapeDtypeStruct((BLOCK, own.shape[1]), jnp.bfloat16),
        in_specs=[SMEM] + [VMEM] * (1 + len(parts)),
        out_specs=VMEM,
        compiler_params=pltpu.CompilerParams(vmem_limit_bytes=16 << 20),
    )(meta, own, *parts)


def along_ring(x, step):
    return lax.ppermute(x, RING, [(i, (i + step) % N_RING) for i in range(N_RING)])


def to_group(x, step):
    return lax.ppermute(x, GROUP, [(i, i + step) for i in range(N_GROUPS) if 0 <= i + step < N_GROUPS])


def shards(queries, keys, values, doc_lengths):
    rows = queries.shape[0]
    kv_heads = keys.shape[1] // HEAD
    by_head = jnp.concatenate([x.reshape(rows, kv_heads, -1) for x in (queries, keys, values)], axis=2)
    mine = lax.all_to_all(by_head.reshape(rows, -1), "kvh", split_axis=1, concat_axis=0, tiled=True)
    width = queries.shape[1] // kv_heads
    q, kv = mine[:, :width], mine[:, width:]
    g, z = lax.axis_index(GROUP), lax.axis_index(RING)
    meta = jnp.concatenate([jnp.stack([g, z]).astype(jnp.int32), doc_lengths])

    half = BLOCK // 2
    visiting = {}
    blocks, up, down = [kv], kv, kv
    for step in range(3):
        up, down = along_ring(up, 1), along_ring(down, -1)
        blocks += [up, down]
    blocks.append(along_ring(up, 1))
    for d in range(1, REACH + 1):
        visiting[d] = to_group(q, -d)
    held = assemble_call(meta, (0, 1, 7, 2, 6, 3), blocks[:6])
    k, v = assemble_call(meta, (5, 4), blocks[6:], *held)
    parts = {}
    first = blocks[0][:half]
    for r, i in enumerate((1, 3, 5, 7, 6, 4, 2), 1):
        first = jnp.where(z == r, blocks[i][:half], first)
    order = (1, 2, 3, 4)
    for turn, d in enumerate(order):
        part = attend_call(d, meta, visiting[d], k, v)
        if turn == 1:
            part, first = lax.optimization_barrier((part, first))
            sink = jnp.zeros_like(first)
            for far in range(REACH + 1, N_GROUPS):
                sink = jnp.where(g == far, lax.ppermute(first, GROUP, [(0, far)]), sink)
        parts[d] = to_group(part, d)
    own = attend_call(0, meta, q, k, v, sink)
    parts = [parts[d] for d in range(1, REACH + 1)]
    out = merge_call(meta, own, parts)
    return lax.all_to_all(out, "kvh", split_axis=0, concat_axis=1, tiled=True)


def solution(mesh):
    torus = Mesh(mesh.devices.reshape(2, 4, 8, mesh.shape["kvh"]), CTX_KVH)
    in_specs = (P(CTX_KVH, None), P(CTX_KVH, None), P(CTX_KVH, None), P())
    return jax.shard_map(
        shards, mesh=torus, in_specs=in_specs, out_specs=P(CTX_KVH, None), check_vma=False
    )
```
